256 devices in a mesh: cfg: 2 (over x_lo), seq: 128 (over y, z, x_hi, core).
Axes of the slice: x: 4 (x_hi: 2, x_lo: 2; x = x_hi * 2 + x_lo), y: 4, z: 8, core: 2. Of those that a mesh axis runs over, the one named last changes fastest.
Arguments:
- queries: bfloat16 [2, 4608, 1536], P('cfg', 'seq'), may hold values from -25 to 25
- keys: bfloat16 [2, 4608, 1536], P('cfg', 'seq'), may hold values from -25 to 25
- values: bfloat16 [2, 4608, 1536], P('cfg', 'seq'), may hold values from -6 to 6
- residual: bfloat16 [2, 4608, 3072], P('cfg', 'seq'), may hold values from -4 to 4
- gate: float32 [2, 3072], P('cfg'), may hold values from 0.5 to 4
- text_len: int32 [2], P('cfg'), may hold values from 64 to 512
- w_out: bfloat16 [1536, 3072], replicated, may hold values from -0.15625 to 0.15625
- w_final: bfloat16 [3072, 64], replicated, may hold values from -0.109375 to 0.109375
- latent: float32 [128, 2048], P('seq', 'cfg'), may hold values from -6 to 6
- owner: int32 [128], replicated, may hold values from 0 to 127, as said below
Outputs:
- hidden_out: bfloat16 [2, 4608, 3072], P('cfg', 'seq')
- latent_next: float32 [128, 2048], P('seq', 'cfg')
The draws below stay inside these ranges and needn't reach their ends.
Inputs may be any that keep to these rules, and one draw needn't show every extreme that they name: `owner`: a permutation of the indices of seq.
All inputs are finite; a program needn't handle non-finite values.
Results may differ from the reference program's by a relative error of at most 0.0065.
Values may be sent and summed in bfloat16 or wider, within the bound.
A program may use at most 192 MiB of HBM per device.

```python
import math
import jax
import jax.numpy as jnp
from jax import lax

D = 3072
HEADS = 12
HEAD = 128
CH = 64
TOK_DEV = 36
W = 1536
SEQ = 4608
TXT = 512
TILE = 32
N_SEQ = 128


def draw_queries(key, part):
    drawn = 2.0 * jax.random.truncated_normal(jax.random.fold_in(key, 1), -5.0, 5.0, (2, SEQ, W), jnp.float32)
    return drawn.astype(jnp.bfloat16)


def draw_keys(key, part):
    drawn = jax.random.truncated_normal(jax.random.fold_in(key, 2), -5.0, 5.0, (2, SEQ, W), jnp.float32)
    return drawn.astype(jnp.bfloat16)


def draw_owner(key, part):
    order = jax.random.permutation(jax.random.fold_in(key, 21), N_SEQ).astype(jnp.int32)
    picked = jax.random.randint(jax.random.fold_in(key, 22), (), 0, N_SEQ, dtype=jnp.int32)
    index = jnp.arange(N_SEQ, dtype=jnp.int32)
    middle = (TXT + picked * TILE + TILE // 2) // TOK_DEV
    target = ((middle + N_SEQ // 2) % N_SEQ).astype(jnp.int32)
    target_at = jnp.sum(jnp.where(order == target, index, 0)).astype(jnp.int32)
    current = jnp.sum(jnp.where(index == picked, order, 0)).astype(jnp.int32)
    order = jnp.where(index == picked, target, jnp.where(index == target_at, current, order))
    return order.astype(jnp.int32)


def level_of(own_key, dims, pieces, least, top_value):
    def one(axis_at, parts):
        steps = jax.random.uniform(jax.random.fold_in(jax.random.fold_in(own_key, 6), axis_at), (parts,), jnp.float32, least / len(pieces), top_value / len(pieces))
        return jnp.repeat(jnp.exp(steps), dims[axis_at] // parts).reshape((-1,) + (1,) * (len(dims) - axis_at - 1))

    factor_of = one(*pieces[0])
    for cut in pieces[1:]:
        factor_of = factor_of * one(*cut)
    return factor_of


def noise(stream_key, shape, scale, most, pieces=(), held_as=jnp.bfloat16):
    values = jax.random.normal(stream_key, shape, jnp.float32) * scale
    if len(pieces) > 0:
        values = level_of(stream_key, shape, pieces, -0.22, 0.18) * values
    return jnp.clip(values, min=-most, max=most).astype(held_as)


def setup_inputs(seed: int = 0) -> dict:
    key_of = jax.random.split(jax.random.key(seed), 11)
    queries = draw_queries(jax.random.fold_in(key_of[10], 71), 0)
    keys = draw_keys(jax.random.fold_in(key_of[10], 71), 0)
    values = noise(key_of[2], (2, SEQ, W), 1.0, 6.0, ((0, 2), (1, 128)))
    residual = noise(key_of[3], (2, SEQ, D), 0.5, 4.0, ((0, 2), (1, 128)))
    gate = jnp.clip(jnp.exp(math.log(4.0) - 2.0794415 * jax.random.uniform(key_of[4], (2, D), jnp.float32) ** level_of(key_of[4], (2, D), ((0, 2),), -0.2, 0.2)), 0.5, 4.0)
    text_len = jax.random.randint(key_of[5], (2,), TXT // 8, TXT + 1).astype(jnp.int32)
    w_out = noise(key_of[6], (W, D), W ** -0.5, 0.15625)
    w_final = noise(key_of[7], (D, CH), D ** -0.5, 0.109375)
    latent = noise(key_of[8], (N_SEQ, TILE * CH), 1.0, 6.0, ((0, 128), (1, 2)), jnp.float32)
    owner = draw_owner(jax.random.fold_in(key_of[10], 71), 0)
    return dict(queries=queries, keys=keys, values=values, residual=residual, gate=gate, text_len=text_len, w_out=w_out, w_final=w_final, latent=latent, owner=owner)


def attend(query, key_all, value_all, limit):
    keypos = jnp.arange(SEQ, dtype=jnp.int32)
    valid = (keypos >= TXT) | (keypos < limit)
    qh = query.reshape(SEQ, HEADS, HEAD).transpose(1, 0, 2)
    kh = key_all.reshape(SEQ, HEADS, HEAD).transpose(1, 0, 2)
    vh = value_all.reshape(SEQ, HEADS, HEAD).transpose(1, 0, 2)
    scale = HEAD ** -0.5

    def one_head(items):
        qq, kk, vv = items
        scores = jnp.dot(qq, kk.T, preferred_element_type=jnp.float32) * scale
        scores = jnp.where(valid[None, :], scores, -1e30)
        top = jnp.max(scores, axis=1, keepdims=True)
        expo = jnp.where(valid[None, :], jnp.exp(scores - top), 0.0)
        total = jnp.sum(expo, axis=1, keepdims=True)
        numer = jnp.dot(expo.astype(jnp.bfloat16), vv, preferred_element_type=jnp.float32)
        return (numer / total).astype(jnp.bfloat16)

    out = lax.map(one_head, (qh, kh, vh))
    return out.transpose(1, 0, 2).reshape(SEQ, W)


def reference(queries, keys, values, residual, gate, text_len, w_out, w_final, latent, owner):
    streams = []
    speeds = []
    for half in range(2):
        attn = attend(queries[half], keys[half], values[half], text_len[half])
        proj = jnp.dot(attn, w_out, preferred_element_type=jnp.float32)
        out = (residual[half].astype(jnp.float32) + gate[half][None, :] * proj).astype(jnp.bfloat16)
        streams.append(out)
        speeds.append(jnp.dot(out, w_final, preferred_element_type=jnp.float32))
    guided = speeds[1] + 3.0 * (speeds[0] - speeds[1])
    tiles = guided[TXT:].reshape(N_SEQ, TILE * CH)
    placed = jnp.zeros((N_SEQ, TILE * CH), jnp.float32).at[owner].set(tiles)
    latent_next = latent - 0.25 * placed
    return jnp.stack(streams), latent_next
```

```python
import jax
import jax.numpy as jnp
from jax import lax
from jax.sharding import PartitionSpec as P

HEADS = 12
HEAD = 128
CH = 64


def partner_2(x, axis, distance):
    return lax.ppermute(x, axis, [(i, i ^ 1 << distance) for i in range(lax.axis_size(axis))])


def local(queries, keys, values, residual, gate, text_len, w_out, w_final, latent, owner):
    qloc = queries[0]
    kloc = keys[0]
    vloc = values[0]
    tokens, width = qloc.shape
    nseq = lax.axis_size("seq")
    myself = lax.axis_index("seq")
    seqlen = tokens * nseq
    textslots = seqlen // 9
    limit = text_len[0]
    scale = HEAD ** (-0.5)
    both = lax.all_gather(jnp.concatenate([kloc, vloc], axis=1), "seq", axis=0, tiled=True)
    qheads = qloc.reshape(tokens, HEADS, HEAD)
    kall = both[:, :width].reshape(seqlen, HEADS, HEAD)
    vall = both[:, width:].reshape(seqlen, HEADS, HEAD)
    keypos = jnp.arange(seqlen, dtype=jnp.int32)
    valid = (keypos >= textslots) | (keypos < limit)
    scores = jnp.einsum("qhd,khd->hqk", qheads, kall, preferred_element_type=jnp.float32) * scale
    scores = jnp.where(valid[None, None, :], scores, -1e30)
    top = jnp.max(scores, axis=2, keepdims=True)
    expo = jnp.where(valid[None, None, :], jnp.exp(scores - top), 0.0)
    total = jnp.sum(expo, axis=2, keepdims=True)
    accum = jnp.einsum(
        "hqk,khd->hqd", expo.astype(jnp.bfloat16), vall, preferred_element_type=jnp.float32
    )
    attn = (accum / total).astype(jnp.bfloat16).transpose(1, 0, 2).reshape(tokens, width)
    proj = jnp.dot(attn, w_out, preferred_element_type=jnp.float32)
    stream = (residual[0].astype(jnp.float32) + gate[0][None, :] * proj).astype(jnp.bfloat16)
    is_cond = lax.axis_index("cfg") == 0
    speed = jnp.dot(stream, w_final, preferred_element_type=jnp.float32)
    other = partner_2(speed, "cfg", 0)
    speed_cond = jnp.where(is_cond, speed, other)
    speed_free = jnp.where(is_cond, other, speed)
    guided = speed_free + 3.0 * (speed_cond - speed_free)
    gathered = lax.all_gather(guided, "seq", axis=0, tiled=True)
    columns = latent.shape[1]
    tilerows = columns * lax.axis_size("cfg") // CH
    mytile = jnp.sum(jnp.where(owner == myself, jnp.arange(nseq, dtype=jnp.int32), 0))
    picked = lax.dynamic_slice_in_dim(gathered, textslots + mytile * tilerows, tilerows, 0)
    flat = picked.reshape(tilerows * CH)
    mine = lax.dynamic_slice_in_dim(flat, lax.axis_index("cfg") * columns, columns, 0)
    latent_next = latent - 0.25 * mine.reshape(1, columns)
    return (stream[None], latent_next)


def solution(mesh):
    placed = (
        P("cfg", "seq", None),
        P("cfg", "seq", None),
        P("cfg", "seq", None),
        P("cfg", "seq", None),
        P("cfg", None),
        P("cfg"),
        P(),
        P(),
        P("seq", "cfg"),
        P(),
    )
    return jax.shard_map(
        local,
        mesh=mesh,
        in_specs=placed,
        out_specs=(P("cfg", "seq", None), P("seq", "cfg")),
        check_vma=False,
    )
```

```python
import functools
import math

import jax
import jax.numpy as jnp
from jax import lax
from jax.experimental import pallas as pl
from jax.experimental.pallas import tpu as pltpu
from jax.sharding import PartitionSpec as P

HEADS = 12
HEAD = 128
CH = 64
RING = 4
PLANES = 8
GROUPS = 4
MINE = HEADS // GROUPS
MESH = pl.DeviceIdType.MESH
NEG = -1e30

ORDER = [(0, 0), (3, 0), (1, 0), (0, 3), (0, 1), (2, 0), (3, 3), (3, 1)]
ORDER += [(1, 3), (1, 1), (0, 2), (2, 3), (2, 1), (3, 2), (1, 2), (2, 2)]
READY = {ab: max(ORDER.index(ab), ORDER.index(ab[::-1])) for ab in ORDER}
SLOT = {ab: p for p, ab in enumerate(sorted(ORDER, key=lambda ab: (READY[ab], ORDER.index(ab))))}
BLOCKS = sorted(ORDER, key=lambda ab: SLOT[ab])
PER = 4


def attention_kernel(
    text_slots,
    limit_ref,
    q_ref,
    k_ref,
    v_ref,
    residual_ref,
    gate_ref,
    w_out_ref,
    w_final_ref,
    hidden_ref,
    guided_ref,
    w_out,
    limit_own,
    limit_in,
    q_in,
    k_in,
    v_in,
    wide,
    q_all,
    k_all,
    v_all,
    top,
    total,
    accum,
    o_out,
    attn,
    speed,
    speed_in,
    w_sem,
    send_sem,
    in_sem,
    self_sem,
    k_sem,
    v_sem,
    k_pair_sem,
    v_pair_sem,
    o_sem,
    speed_sem,
):
    rows = q_ref.shape[0]
    cols = MINE * HEAD
    keys = RING * rows
    cut = (keys // 2 + 15) // 16 * 16
    cfg = lax.axis_index("cfg")
    seq = lax.axis_index("seq")
    core = lax.rem(seq, 2)
    xh = lax.rem(seq // 2, 2)
    z = lax.rem(seq // 4, PLANES)
    y = seq // (4 * PLANES)
    x = 2 * xh + cfg
    half = lax.rem(z, 2)
    group = z // 2

    def device(x_at, y_at, z_at, core_at):
        return (lax.rem(x_at, 2), ((y_at * PLANES + z_at) * 2 + x_at // 2) * 2 + core_at)

    def peer(j):
        return device(2 * xh + half, y, 2 * j + cfg, core)

    def beside(axis, step):
        if axis == 0:
            return device(lax.rem(x + step + RING, RING), y, z, core)
        return device(x, lax.rem(y + step + RING, RING), z, core)

    partner = device(x, y, z, 1 - core)
    at_home = cfg == half

    w_copy = pltpu.make_async_copy(w_out_ref, w_out, w_sem)
    w_copy.start()
    limit_own[...] = jnp.full(limit_own.shape, limit_ref[0], jnp.int32)

    barrier = pltpu.get_barrier_semaphore()
    for j in range(GROUPS):
        mine = at_home & (group == j)

        @pl.when(jnp.logical_not(mine))
        def _():
            pl.semaphore_signal(barrier, inc=1, device_id=peer(j), device_id_type=MESH)

    for other in (beside(0, 1), beside(0, -1), beside(1, 1), beside(1, -1), partner):
        pl.semaphore_signal(barrier, inc=1, device_id=other, device_id_type=MESH)
    pl.semaphore_wait(barrier, jnp.where(at_home, GROUPS + 4, GROUPS + 5))

    sent = []

    def send(src, dst, arrival, where):
        copy = pltpu.make_async_remote_copy(
            src_ref=src,
            dst_ref=dst,
            send_sem=send_sem.at[len(sent)],
            recv_sem=arrival,
            device_id=where,
            device_id_type=MESH,
        )
        copy.start()
        sent.append(copy)

    spread = []

    def scatter(src, dst, arrival, j, at):
        mine = at_home & (group == j)
        remote = pltpu.make_async_remote_copy(
            src_ref=src,
            dst_ref=dst,
            send_sem=self_sem.at[at],
            recv_sem=arrival,
            device_id=peer(j),
            device_id_type=MESH,
        )
        local = pltpu.make_async_copy(src, dst, arrival)

        @pl.when(mine)
        def _():
            local.start()

        @pl.when(jnp.logical_not(mine))
        def _():
            remote.start()

        spread.append((mine, remote))

    def arrived(ref, sem):
        pltpu.make_async_copy(ref, ref, sem).wait()

    packs = ((k_ref, k_in), (v_ref, v_in), (q_ref, q_in))
    for t, (src, dst) in enumerate(packs):
        for g in range(GROUPS):
            scatter(
                src.at[:, pl.ds(g * cols, cols)],
                dst.at[group],
                in_sem.at[t, group],
                g,
                t * GROUPS + g,
            )
    for g in range(GROUPS):
        scatter(limit_own, limit_in.at[group], in_sem.at[3, group], g, 3 * GROUPS + g)

    def compact(t, landed):
        for j in range(RING):
            arrived(landed.at[j], in_sem.at[t, j])
            wide[pl.ds(j * rows, rows), :] = landed[j].astype(jnp.float32)
        return wide[...].astype(jnp.bfloat16)

    def place(ab, values):
        return SLOT[ab[::-1]] if values else SLOT[ab]

    def have(ab, values):
        a, b = ab
        store, arrive, pair = (v_all, v_sem, v_pair_sem) if values else (k_all, k_sem, k_pair_sem)
        first, second = (1, 0) if values else (0, 1)
        p = place(ab, values)

        def whole(axis, step, to):
            s = place(to, values)
            send(store.at[2 * p], store.at[2 * s], arrive.at[s, 0], beside(axis, step))

        def part(axis, step, to, which):
            s = place(to, values)
            span = pl.ds(0, cut) if which == 0 else pl.ds(cut, keys - cut)
            send(
                store.at[2 * p, span],
                store.at[2 * s, span],
                arrive.at[s, which],
                beside(axis, step),
            )

        if b == 0:
            if a == 0:
                whole(first, 1, (3, 0))
                whole(first, -1, (1, 0))
            if a == 3:
                part(first, 1, (2, 0), 0)
            if a == 1:
                part(first, -1, (2, 0), 1)
            whole(second, 1, (a, 3))
            whole(second, -1, (a, 1))
        if b == 3:
            part(second, 1, (a, 2), 0)
        if b == 1:
            part(second, -1, (a, 2), 1)
        send(store.at[2 * p], store.at[2 * p + 1], pair.at[p], partner)

    def await_block(ab, values):
        a, b = ab
        store, arrive = (v_all, v_sem) if values else (k_all, k_sem)
        p = place(ab, values)
        if b == 2 or (b == 0 and a == 2):
            arrived(store.at[2 * p, pl.ds(0, cut)], arrive.at[p, 0])
            arrived(store.at[2 * p, pl.ds(cut, keys - cut)], arrive.at[p, 1])
        else:
            arrived(store.at[2 * p], arrive.at[p, 0])

    k_all[2 * SLOT[(0, 0)]] = compact(0, k_in)
    have((0, 0), False)
    v_all[2 * SLOT[(0, 0)]] = compact(1, v_in)
    have((0, 0), True)
    q_all[...] = compact(2, q_in)
    for j in range(RING):
        arrived(limit_in.at[j], in_sem.at[3, j])

    top[...] = jnp.full(top.shape, NEG, jnp.float32)
    total[...] = jnp.zeros(total.shape, jnp.float32)
    accum[...] = jnp.zeros(accum.shape, jnp.float32)
    factor = HEAD**-0.5 * math.log2(math.e)

    def bias_of(ab, other):
        x_at = lax.rem(x + ab[0], RING)
        y_at = lax.rem(y + ab[1], RING)
        core_at = 1 - core if other else core
        n = lax.broadcasted_iota(jnp.int32, (1, keys), 1)
        j = sum((n >= rows * i).astype(jnp.int32) for i in range(1, RING))
        holder = ((y_at * PLANES + 2 * j + lax.rem(x_at, 2)) * 2 + x_at // 2) * 2 + core_at
        pos = holder * rows + n - rows * j
        limit = limit_in[0, 0:1, :]
        limit = jnp.concatenate([limit, limit[:, : keys - 128]], axis=1)
        return jnp.where((pos >= text_slots) | (pos < limit), 0.0, NEG)

    def fold(at):
        for ab in BLOCKS[at * PER : (at + 1) * PER]:
            p = SLOT[ab]
            if ab != (0, 0) or True:
                arrived(k_all.at[2 * p + 1], k_pair_sem.at[p])
                arrived(v_all.at[2 * p + 1], v_pair_sem.at[p])
        bias = jnp.concatenate(
            [bias_of(ab, o) for ab in BLOCKS[at * PER : (at + 1) * PER] for o in range(2)], axis=1
        )
        span = pl.ds(at * PER * 2, PER * 2)
        many = PER * 2 * keys
        for h in range(MINE):
            lanes = slice(h * HEAD, (h + 1) * HEAD)
            kk = k_all[span, :, lanes].reshape(many, HEAD)
            vv = v_all[span, :, lanes].reshape(many, HEAD)
            scores = lax.dot_general(
                q_all[:, lanes], kk, (((1,), (1,)), ((), ())), preferred_element_type=jnp.float32
            )
            scores = scores * factor + bias
            old = top[h]
            new = jnp.maximum(old, jnp.max(scores, axis=1, keepdims=True))
            expo = jnp.exp2(scores - new[:, :1])
            shrink = jnp.exp2(old - new)
            top[h] = new
            total[h] = total[h] * shrink + jnp.sum(expo, axis=1, keepdims=True)
            accum[h] = accum[h] * shrink + jnp.dot(
                expo.astype(jnp.bfloat16), vv, preferred_element_type=jnp.float32
            )

    done = 0
    for n, ab in enumerate(ORDER):
        if n == 0:
            continue
        await_block(ab, False)
        have(ab, False)
        await_block(ab, True)
        have(ab, True)
        while (done + 1) * PER < len(BLOCKS) and READY[BLOCKS[(done + 1) * PER - 1]] < n:
            fold(done)
            done += 1
    while done * PER < len(BLOCKS):
        fold(done)
        done += 1

    for h in range(MINE):
        wide[:, pl.ds(h * HEAD, HEAD)] = accum[h] / total[h]
    for j in range(RING):
        o_out[j] = wide[pl.ds(j * rows, rows), :].astype(jnp.bfloat16)
    at_cols = pl.ds(pl.multiple_of(group * cols, cols), cols)
    for j in range(RING):
        scatter(o_out.at[j], attn.at[:, at_cols], o_sem.at[group], j, 4 * GROUPS + j)
    w_copy.wait()
    for g in range(GROUPS):
        arrived(attn.at[:, pl.ds(g * cols, cols)], o_sem.at[g])

    width = hidden_ref.shape[1]
    step = 512
    rate = jnp.zeros(speed.shape, jnp.float32)
    for at in range(0, width, step):
        lanes = slice(at, at + step)
        proj = jnp.dot(attn[...], w_out[:, lanes], preferred_element_type=jnp.float32)
        stream = residual_ref[:, lanes].astype(jnp.float32) + gate_ref[:, lanes] * proj
        stream = stream.astype(jnp.bfloat16)
        hidden_ref[:, lanes] = stream
        rate += jnp.dot(stream, w_final_ref[lanes, :], preferred_element_type=jnp.float32)
    speed[...] = rate
    to = beside_cfg = device(2 * xh + 1 - cfg, y, z, core)
    send(speed, speed_in, speed_sem, to)
    arrived(speed_in, speed_sem)
    other = speed_in[...]
    cond = jnp.where(cfg == 0, rate, other)
    free = jnp.where(cfg == 0, other, rate)
    guided_ref[...] = free + 3.0 * (cond - free)

    for copy in sent:
        copy.wait_send()
    for mine, copy in spread:

        @pl.when(jnp.logical_not(mine))
        def _():
            copy.wait_send()


def local(queries, keys, values, residual, gate, text_len, w_out, w_final, latent, owner):
    tokens, width = queries.shape[1:]
    nseq = lax.axis_size("seq")
    myself = lax.axis_index("seq")
    seqlen = tokens * nseq
    textslots = seqlen // 9
    cols = MINE * HEAD
    block = RING * tokens
    vmem = pl.BlockSpec(memory_space=pltpu.VMEM)
    bf16, f32 = jnp.bfloat16, jnp.float32
    dma = pltpu.SemaphoreType.DMA
    stream, guided = pl.pallas_call(
        functools.partial(attention_kernel, textslots),
        out_shape=(
            jax.ShapeDtypeStruct(residual.shape[1:], bf16),
            jax.ShapeDtypeStruct((tokens, CH), f32),
        ),
        in_specs=[pl.BlockSpec(memory_space=pltpu.SMEM)]
        + [vmem] * 5
        + [pl.BlockSpec(memory_space=pl.ANY), vmem],
        out_specs=(vmem, vmem),
        scratch_shapes=[
            pltpu.VMEM(w_out.shape, bf16),
            pltpu.VMEM((8, 128), jnp.int32),
            pltpu.VMEM((RING, 8, 128), jnp.int32),
            pltpu.VMEM((RING, tokens, cols), bf16),
            pltpu.VMEM((RING, tokens, cols), bf16),
            pltpu.VMEM((RING, tokens, cols), bf16),
            pltpu.VMEM((block, cols), f32),
            pltpu.VMEM((block, cols), bf16),
            pltpu.VMEM((2 * len(ORDER), block, cols), bf16),
            pltpu.VMEM((2 * len(ORDER), block, cols), bf16),
            pltpu.VMEM((MINE, block, HEAD), f32),
            pltpu.VMEM((MINE, block, HEAD), f32),
            pltpu.VMEM((MINE, block, HEAD), f32),
            pltpu.VMEM((RING, tokens, cols), bf16),
            pltpu.VMEM((tokens, width), bf16),
            pltpu.VMEM((tokens, CH), f32),
            pltpu.VMEM((tokens, CH), f32),
            dma,
            dma((73,)),
            dma((4, RING)),
            dma((20,)),
            dma((len(ORDER), 2)),
            dma((len(ORDER), 2)),
            dma((len(ORDER),)),
            dma((len(ORDER),)),
            dma((GROUPS,)),
            dma,
        ],
        compiler_params=pltpu.CompilerParams(
            collective_id=0, has_side_effects=True, vmem_limit_bytes=60 * 1024 * 1024
        ),
    )(text_len, queries[0], keys[0], values[0], residual[0], gate, w_out, w_final)
    gathered = lax.all_gather(guided, "seq", axis=0, tiled=True)
    columns = latent.shape[1]
    tilerows = columns * lax.axis_size("cfg") // CH
    mytile = jnp.sum(jnp.where(owner == myself, jnp.arange(nseq, dtype=jnp.int32), 0))
    picked = lax.dynamic_slice_in_dim(gathered, textslots + mytile * tilerows, tilerows, 0)
    flat = picked.reshape(tilerows * CH)
    mine = lax.dynamic_slice_in_dim(flat, lax.axis_index("cfg") * columns, columns, 0)
    latent_next = latent - 0.25 * mine.reshape(1, columns)
    return (stream[None], latent_next)


def solution(mesh):
    placed = (
        P("cfg", "seq", None),
        P("cfg", "seq", None),
        P("cfg", "seq", None),
        P("cfg", "seq", None),
        P("cfg", None),
        P("cfg"),
        P(),
        P(),
        P("seq", "cfg"),
        P(),
    )
    return jax.shard_map(
        local,
        mesh=mesh,
        in_specs=placed,
        out_specs=(P("cfg", "seq", None), P("seq", "cfg")),
        check_vma=False,
    )
```

```python
import functools
import math

import jax
import jax.numpy as jnp
from jax import lax
from jax.experimental import pallas as pl
from jax.experimental.pallas import tpu as pltpu
from jax.sharding import PartitionSpec as P

HEADS = 12
HEAD = 128
CH = 64
RING = 4
PLANES = 8
GROUPS = 4
MINE = HEADS // GROUPS
MESH = pl.DeviceIdType.MESH
NEG = -1e30

ORDER = [(0, 0), (3, 0), (1, 0), (0, 3), (0, 1), (2, 0), (3, 3), (3, 1)]
ORDER += [(1, 3), (1, 1), (0, 2), (2, 3), (2, 1), (3, 2), (1, 2), (2, 2)]
READY = {ab: max(ORDER.index(ab), ORDER.index(ab[::-1])) for ab in ORDER}
SLOT = {ab: p for p, ab in enumerate(sorted(ORDER, key=lambda ab: (READY[ab], ORDER.index(ab))))}
BLOCKS = sorted(ORDER, key=lambda ab: SLOT[ab])
PER = 4
PART = 16


def attention_kernel(
    text_slots,
    limit_ref,
    tile_ref,
    q_ref,
    k_ref,
    v_ref,
    residual_ref,
    gate_ref,
    w_out_ref,
    w_final_ref,
    hidden_ref,
    mine_ref,
    w_out,
    limit_own,
    limit_in,
    q_in,
    k_in,
    v_in,
    wide,
    q_all,
    k_all,
    v_all,
    top,
    total,
    accum,
    o_out,
    attn,
    speed,
    speed_in,
    aligned,
    tiles,
    w_sem,
    send_sem,
    in_sem,
    self_sem,
    k_sem,
    v_sem,
    k_pair_sem,
    v_pair_sem,
    o_sem,
    speed_sem,
    x_sem,
    z_sem,
    y_sem,
    core_sem,
):
    rows = q_ref.shape[0]
    cols = MINE * HEAD
    keys = RING * rows
    cut = (keys // 2 + 15) // 16 * 16
    cfg = lax.axis_index("cfg")
    seq = lax.axis_index("seq")
    core = lax.rem(seq, 2)
    xh = lax.rem(seq // 2, 2)
    z = lax.rem(seq // 4, PLANES)
    y = seq // (4 * PLANES)
    x = 2 * xh + cfg
    half = lax.rem(z, 2)
    group = z // 2

    def device(x_at, y_at, z_at, core_at):
        return (lax.rem(x_at, 2), ((y_at * PLANES + z_at) * 2 + x_at // 2) * 2 + core_at)

    def peer(j):
        return device(2 * xh + half, y, 2 * j + cfg, core)

    def beside(axis, step):
        if axis == 0:
            return device(lax.rem(x + step + RING, RING), y, z, core)
        return device(x, lax.rem(y + step + RING, RING), z, core)

    partner = device(x, y, z, 1 - core)
    at_home = cfg == half

    w_copy = pltpu.make_async_copy(w_out_ref, w_out, w_sem)
    w_copy.start()
    limit_own[...] = jnp.full(limit_own.shape, limit_ref[0], jnp.int32)

    barrier = pltpu.get_barrier_semaphore()
    for j in range(GROUPS):
        mine = at_home & (group == j)

        @pl.when(jnp.logical_not(mine))
        def _():
            pl.semaphore_signal(barrier, inc=1, device_id=peer(j), device_id_type=MESH)

    across = device(lax.rem(x + 2, RING), y, z, core)
    planes = [device(x, y, lax.rem(z + d, PLANES), core) for d in range(1, PLANES)]
    others = [beside(0, 1), beside(0, -1), beside(1, 1), beside(1, -1), partner]
    others += [across, beside(1, 2)] + planes
    for other in others:
        pl.semaphore_signal(barrier, inc=1, device_id=other, device_id_type=MESH)
    pl.semaphore_wait(barrier, GROUPS + len(others) - at_home.astype(jnp.int32))

    sent = []

    def send(src, dst, arrival, where):
        copy = pltpu.make_async_remote_copy(
            src_ref=src,
            dst_ref=dst,
            send_sem=send_sem.at[len(sent)],
            recv_sem=arrival,
            device_id=where,
            device_id_type=MESH,
        )
        copy.start()
        sent.append(copy)

    spread = []

    def scatter(src, dst, arrival, j, at):
        mine = at_home & (group == j)
        remote = pltpu.make_async_remote_copy(
            src_ref=src,
            dst_ref=dst,
            send_sem=self_sem.at[at],
            recv_sem=arrival,
            device_id=peer(j),
            device_id_type=MESH,
        )
        local = pltpu.make_async_copy(src, dst, arrival)

        @pl.when(mine)
        def _():
            local.start()

        @pl.when(jnp.logical_not(mine))
        def _():
            remote.start()

        spread.append((mine, remote))

    def arrived(ref, sem):
        pltpu.make_async_copy(ref, ref, sem).wait()

    packs = ((k_ref, k_in), (v_ref, v_in), (q_ref, q_in))
    for t, (src, dst) in enumerate(packs):
        for g in range(GROUPS):
            scatter(
                src.at[:, pl.ds(g * cols, cols)],
                dst.at[group],
                in_sem.at[t, group],
                g,
                t * GROUPS + g,
            )
    for g in range(GROUPS):
        scatter(limit_own, limit_in.at[group], in_sem.at[3, group], g, 3 * GROUPS + g)

    def compact(t, landed):
        for j in range(RING):
            arrived(landed.at[j], in_sem.at[t, j])
            wide[pl.ds(j * rows, rows), :] = landed[j].astype(jnp.float32)
        return wide[...].astype(jnp.bfloat16)

    def place(ab, values):
        return SLOT[ab[::-1]] if values else SLOT[ab]

    def have(ab, values):
        a, b = ab
        store, arrive, pair = (v_all, v_sem, v_pair_sem) if values else (k_all, k_sem, k_pair_sem)
        first, second = (1, 0) if values else (0, 1)
        p = place(ab, values)

        def whole(axis, step, to):
            s = place(to, values)
            send(store.at[2 * p], store.at[2 * s], arrive.at[s, 0], beside(axis, step))

        def part(axis, step, to, which):
            s = place(to, values)
            span = pl.ds(0, cut) if which == 0 else pl.ds(cut, keys - cut)
            send(
                store.at[2 * p, span],
                store.at[2 * s, span],
                arrive.at[s, which],
                beside(axis, step),
            )

        if b == 0:
            if a == 0:
                whole(first, 1, (3, 0))
                whole(first, -1, (1, 0))
            if a == 3:
                part(first, 1, (2, 0), 0)
            if a == 1:
                part(first, -1, (2, 0), 1)
            whole(second, 1, (a, 3))
            whole(second, -1, (a, 1))
        if b == 3:
            part(second, 1, (a, 2), 0)
        if b == 1:
            part(second, -1, (a, 2), 1)
        send(store.at[2 * p], store.at[2 * p + 1], pair.at[p], partner)

    def await_block(ab, values):
        a, b = ab
        store, arrive = (v_all, v_sem) if values else (k_all, k_sem)
        p = place(ab, values)
        if b == 2 or (b == 0 and a == 2):
            arrived(store.at[2 * p, pl.ds(0, cut)], arrive.at[p, 0])
            arrived(store.at[2 * p, pl.ds(cut, keys - cut)], arrive.at[p, 1])
        else:
            arrived(store.at[2 * p], arrive.at[p, 0])

    k_all[2 * SLOT[(0, 0)]] = compact(0, k_in)
    have((0, 0), False)
    v_all[2 * SLOT[(0, 0)]] = compact(1, v_in)
    have((0, 0), True)
    q_all[...] = compact(2, q_in)
    for j in range(RING):
        arrived(limit_in.at[j], in_sem.at[3, j])

    top[...] = jnp.full(top.shape, NEG, jnp.float32)
    total[...] = jnp.zeros(total.shape, jnp.float32)
    accum[...] = jnp.zeros(accum.shape, jnp.float32)
    factor = HEAD**-0.5 * math.log2(math.e)

    def bias_of(ab, other):
        x_at = lax.rem(x + ab[0], RING)
        y_at = lax.rem(y + ab[1], RING)
        core_at = 1 - core if other else core
        n = lax.broadcasted_iota(jnp.int32, (1, keys), 1)
        j = sum((n >= rows * i).astype(jnp.int32) for i in range(1, RING))
        holder = ((y_at * PLANES + 2 * j + lax.rem(x_at, 2)) * 2 + x_at // 2) * 2 + core_at
        pos = holder * rows + n - rows * j
        limit = limit_in[0, 0:1, :]
        limit = jnp.concatenate([limit, limit[:, : keys - 128]], axis=1)
        return jnp.where((pos >= text_slots) | (pos < limit), 0.0, NEG)

    def fold(at):
        for ab in BLOCKS[at * PER : (at + 1) * PER]:
            p = SLOT[ab]
            if ab != (0, 0) or True:
                arrived(k_all.at[2 * p + 1], k_pair_sem.at[p])
                arrived(v_all.at[2 * p + 1], v_pair_sem.at[p])
        bias = jnp.concatenate(
            [bias_of(ab, o) for ab in BLOCKS[at * PER : (at + 1) * PER] for o in range(2)], axis=1
        )
        span = pl.ds(at * PER * 2, PER * 2)
        many = PER * 2 * keys
        for h in range(MINE):
            lanes = slice(h * HEAD, (h + 1) * HEAD)
            kk = k_all[span, :, lanes].reshape(many, HEAD)
            vv = v_all[span, :, lanes].reshape(many, HEAD)
            scores = lax.dot_general(
                q_all[:, lanes], kk, (((1,), (1,)), ((), ())), preferred_element_type=jnp.float32
            )
            scores = scores * factor + bias
            old = top[h]
            new = jnp.maximum(old, jnp.max(scores, axis=1, keepdims=True))
            expo = jnp.exp2(scores - new[:, :1])
            shrink = jnp.exp2(old - new)
            top[h] = new
            total[h] = total[h] * shrink + jnp.sum(expo, axis=1, keepdims=True)
            accum[h] = accum[h] * shrink + jnp.dot(
                expo.astype(jnp.bfloat16), vv, preferred_element_type=jnp.float32
            )

    done = 0
    for n, ab in enumerate(ORDER):
        if n == 0:
            continue
        await_block(ab, False)
        have(ab, False)
        await_block(ab, True)
        have(ab, True)
        while (done + 1) * PER < len(BLOCKS) and READY[BLOCKS[(done + 1) * PER - 1]] < n:
            fold(done)
            done += 1
    while done * PER < len(BLOCKS):
        fold(done)
        done += 1

    for h in range(MINE):
        wide[:, pl.ds(h * HEAD, HEAD)] = accum[h] / total[h]
    for j in range(RING):
        o_out[j] = wide[pl.ds(j * rows, rows), :].astype(jnp.bfloat16)
    at_cols = pl.ds(pl.multiple_of(group * cols, cols), cols)
    for j in range(RING):
        scatter(o_out.at[j], attn.at[:, at_cols], o_sem.at[group], j, 4 * GROUPS + j)
    w_copy.wait()
    for g in range(GROUPS):
        arrived(attn.at[:, pl.ds(g * cols, cols)], o_sem.at[g])

    width = hidden_ref.shape[1]
    step = 512
    rate = jnp.zeros(speed.shape, jnp.float32)
    for at in range(0, width, step):
        lanes = slice(at, at + step)
        proj = jnp.dot(attn[...], w_out[:, lanes], preferred_element_type=jnp.float32)
        stream = residual_ref[:, lanes].astype(jnp.float32) + gate_ref[:, lanes] * proj
        stream = stream.astype(jnp.bfloat16)
        hidden_ref[:, lanes] = stream
        rate += jnp.dot(stream, w_final_ref[lanes, :], preferred_element_type=jnp.float32)
    speed[...] = rate
    to = device(2 * xh + 1 - cfg, y, z, core)
    send(speed, speed_in, speed_sem, to)
    arrived(speed_in, speed_sem)
    other = speed_in[...]
    cond = jnp.where(cfg == 0, rate, other)
    free = jnp.where(cfg == 0, other, rate)
    aligned[...] = jnp.zeros(aligned.shape, jnp.float32)
    aligned[pl.ds(0, rows), pl.ds(0, CH)] = free + 3.0 * (cond - free)
    rolled = pltpu.roll(aligned[...], lax.rem(rows * seq, 2 * PART), 0)
    parts = [rolled[i * PART : (i + 1) * PART] for i in range(4)]
    near = jnp.where(cfg == 0, parts[0], parts[1])
    far = jnp.where(cfg == 0, parts[2], parts[3])
    each = PLANES * 2
    base = core * RING * each
    own = base + seq // 2
    tiles[own] = near + pltpu.roll(far, CH, 1)

    send(tiles.at[own], tiles.at[own], x_sem, across)
    arrived(tiles.at[base + y * each + 2 * z + 1 - xh], x_sem)
    both = tiles.at[pl.ds(base + y * each + 2 * z, 2)]
    for d, where in enumerate(planes):
        send(both, both, z_sem.at[d], where)
    for d in range(1, PLANES):
        z_at = lax.rem(z - d + PLANES, PLANES)
        arrived(tiles.at[pl.ds(base + y * each + 2 * z_at, 2)], z_sem.at[d - 1])
    plane = tiles.at[pl.ds(base + y * each, each)]
    for d in (2, 1, 3):
        send(plane, plane, y_sem.at[d], beside(1, d))
    send(plane, plane, core_sem.at[0], partner)
    for d in (1, 3, 2):
        y_at = lax.rem(y - d + RING, RING)
        plane = tiles.at[pl.ds(base + y_at * each, each)]
        arrived(plane, y_sem.at[d])
        send(plane, plane, core_sem.at[d], partner)
    for d in range(RING):
        y_at = lax.rem(y - d + RING, RING)
        arrived(tiles.at[pl.ds((1 - core) * RING * each + y_at * each, each)], core_sem.at[d])

    tile = text_slots // (2 * PART) + tile_ref[0]
    first = tile * 2 * PART + PART * cfg

    def held(block):
        got = tiles[lax.rem(block, 2) * RING * each + block // 2]
        late = tile - rows * block // (2 * PART)
        return jnp.where(late == 0, got, pltpu.roll(got, CH, 1))

    begin = first // rows
    end = (first + PART - 1) // rows
    picked = held(begin)
    picked += jnp.where(end == begin, jnp.zeros_like(picked), held(end))
    mine_ref[...] = picked[:, :CH]

    for copy in sent:
        copy.wait_send()
    for mine, copy in spread:

        @pl.when(jnp.logical_not(mine))
        def _():
            copy.wait_send()


def local(queries, keys, values, residual, gate, text_len, w_out, w_final, latent, owner):
    tokens, width = queries.shape[1:]
    nseq = lax.axis_size("seq")
    myself = lax.axis_index("seq")
    seqlen = tokens * nseq
    textslots = seqlen // 9
    cols = MINE * HEAD
    block = RING * tokens
    vmem = pl.BlockSpec(memory_space=pltpu.VMEM)
    bf16, f32 = jnp.bfloat16, jnp.float32
    dma = pltpu.SemaphoreType.DMA
    tile = jnp.sum(jnp.where(owner == myself, jnp.arange(nseq, dtype=jnp.int32), 0))
    stream, mine = pl.pallas_call(
        functools.partial(attention_kernel, textslots),
        out_shape=(
            jax.ShapeDtypeStruct(residual.shape[1:], bf16),
            jax.ShapeDtypeStruct((PART, CH), f32),
        ),
        in_specs=[pl.BlockSpec(memory_space=pltpu.SMEM)] * 2
        + [vmem] * 5
        + [pl.BlockSpec(memory_space=pl.ANY), vmem],
        out_specs=(vmem, vmem),
        scratch_shapes=[
            pltpu.VMEM(w_out.shape, bf16),
            pltpu.VMEM((8, 128), jnp.int32),
            pltpu.VMEM((RING, 8, 128), jnp.int32),
            pltpu.VMEM((RING, tokens, cols), bf16),
            pltpu.VMEM((RING, tokens, cols), bf16),
            pltpu.VMEM((RING, tokens, cols), bf16),
            pltpu.VMEM((block, cols), f32),
            pltpu.VMEM((block, cols), bf16),
            pltpu.VMEM((2 * len(ORDER), block, cols), bf16),
            pltpu.VMEM((2 * len(ORDER), block, cols), bf16),
            pltpu.VMEM((MINE, block, HEAD), f32),
            pltpu.VMEM((MINE, block, HEAD), f32),
            pltpu.VMEM((MINE, block, HEAD), f32),
            pltpu.VMEM((RING, tokens, cols), bf16),
            pltpu.VMEM((tokens, width), bf16),
            pltpu.VMEM((tokens, CH), f32),
            pltpu.VMEM((tokens, CH), f32),
            pltpu.VMEM((4 * PART, 2 * CH), f32),
            pltpu.VMEM((nseq, PART, 2 * CH), f32),
            dma,
            dma((88,)),
            dma((4, RING)),
            dma((20,)),
            dma((len(ORDER), 2)),
            dma((len(ORDER), 2)),
            dma((len(ORDER),)),
            dma((len(ORDER),)),
            dma((GROUPS,)),
            dma,
            dma,
            dma((PLANES - 1,)),
            dma((RING,)),
            dma((RING,)),
        ],
        compiler_params=pltpu.CompilerParams(
            collective_id=0, has_side_effects=True, vmem_limit_bytes=60 * 1024 * 1024
        ),
    )(text_len, tile.reshape(1), queries[0], keys[0], values[0], residual[0], gate, w_out, w_final)
    latent_next = latent - 0.25 * mine.reshape(latent.shape)
    return (stream[None], latent_next)


def solution(mesh):
    placed = (
        P("cfg", "seq", None),
        P("cfg", "seq", None),
        P("cfg", "seq", None),
        P("cfg", "seq", None),
        P("cfg", None),
        P("cfg"),
        P(),
        P(),
        P("seq", "cfg"),
        P(),
    )
    return jax.shard_map(
        local,
        mesh=mesh,
        in_specs=placed,
        out_specs=(P("cfg", "seq", None), P("seq", "cfg")),
        check_vma=False,
    )
```

```python
import functools
import math

import jax
import jax.numpy as jnp
from jax import lax
from jax.experimental import pallas as pl
from jax.experimental.pallas import tpu as pltpu
from jax.sharding import PartitionSpec as P

HEADS = 12
HEAD = 128
CH = 64
RING = 4
PLANES = 8
GROUPS = 4
MINE = HEADS // GROUPS
MESH = pl.DeviceIdType.MESH
NEG = -1e30

ORDER = [(0, 0), (3, 0), (1, 0), (0, 3), (0, 1), (2, 0), (3, 3), (3, 1)]
ORDER += [(1, 3), (1, 1), (0, 2), (2, 3), (2, 1), (3, 2), (1, 2), (2, 2)]
READY = {ab: max(ORDER.index(ab), ORDER.index(ab[::-1])) for ab in ORDER}
SLOT = {ab: p for p, ab in enumerate(sorted(ORDER, key=lambda ab: (READY[ab], ORDER.index(ab))))}
BLOCKS = sorted(ORDER, key=lambda ab: SLOT[ab])
PER = 4
PART = 16


def attention_kernel(
    text_slots,
    limit_ref,
    owner_ref,
    q_ref,
    k_ref,
    v_ref,
    residual_ref,
    gate_ref,
    w_out_ref,
    w_final_ref,
    latent_ref,
    hidden_ref,
    latent_next_ref,
    w_out,
    limit_own,
    limit_in,
    q_in,
    k_in,
    v_in,
    wide,
    q_all,
    k_all,
    v_all,
    top,
    total,
    accum,
    o_out,
    attn,
    speed,
    speed_in,
    aligned,
    tiles,
    w_sem,
    send_sem,
    in_sem,
    self_sem,
    k_sem,
    v_sem,
    k_pair_sem,
    v_pair_sem,
    o_sem,
    speed_sem,
    x_sem,
    z_sem,
    y_sem,
    core_sem,
):
    rows = q_ref.shape[0]
    cols = MINE * HEAD
    keys = RING * rows
    cut = (keys // 2 + 15) // 16 * 16
    cfg = lax.axis_index("cfg")
    seq = lax.axis_index("seq")
    core = lax.rem(seq, 2)
    xh = lax.rem(seq // 2, 2)
    z = lax.rem(seq // 4, PLANES)
    y = seq // (4 * PLANES)
    x = 2 * xh + cfg
    half = lax.rem(z, 2)
    group = z // 2

    def device(x_at, y_at, z_at, core_at):
        return (lax.rem(x_at, 2), ((y_at * PLANES + z_at) * 2 + x_at // 2) * 2 + core_at)

    def peer(j):
        return device(2 * xh + half, y, 2 * j + cfg, core)

    def beside(axis, step):
        if axis == 0:
            return device(lax.rem(x + step + RING, RING), y, z, core)
        return device(x, lax.rem(y + step + RING, RING), z, core)

    partner = device(x, y, z, 1 - core)
    at_home = cfg == half

    w_copy = pltpu.make_async_copy(w_out_ref, w_out, w_sem)
    w_copy.start()
    limit_own[...] = jnp.full(limit_own.shape, limit_ref[0], jnp.int32)

    barrier = pltpu.get_barrier_semaphore()
    for j in range(GROUPS):
        mine = at_home & (group == j)

        @pl.when(jnp.logical_not(mine))
        def _():
            pl.semaphore_signal(barrier, inc=1, device_id=peer(j), device_id_type=MESH)

    across = device(lax.rem(x + 2, RING), y, z, core)
    planes = [device(x, y, lax.rem(z + d, PLANES), core) for d in range(1, PLANES)]
    others = [beside(0, 1), beside(0, -1), beside(1, 1), beside(1, -1), partner]
    others += [across, beside(1, 2)] + planes
    for other in others:
        pl.semaphore_signal(barrier, inc=1, device_id=other, device_id_type=MESH)
    pl.semaphore_wait(barrier, GROUPS + len(others) - at_home.astype(jnp.int32))

    sent = []

    def send(src, dst, arrival, where):
        copy = pltpu.make_async_remote_copy(
            src_ref=src,
            dst_ref=dst,
            send_sem=send_sem.at[len(sent)],
            recv_sem=arrival,
            device_id=where,
            device_id_type=MESH,
        )
        copy.start()
        sent.append(copy)

    spread = []

    def scatter(src, dst, arrival, j, at):
        mine = at_home & (group == j)
        remote = pltpu.make_async_remote_copy(
            src_ref=src,
            dst_ref=dst,
            send_sem=self_sem.at[at],
            recv_sem=arrival,
            device_id=peer(j),
            device_id_type=MESH,
        )
        local = pltpu.make_async_copy(src, dst, arrival)

        @pl.when(mine)
        def _():
            local.start()

        @pl.when(jnp.logical_not(mine))
        def _():
            remote.start()

        spread.append((mine, remote))

    def arrived(ref, sem):
        pltpu.make_async_copy(ref, ref, sem).wait()

    packs = ((k_ref, k_in), (v_ref, v_in), (q_ref, q_in))
    for t, (src, dst) in enumerate(packs):
        for g in range(GROUPS):
            scatter(
                src.at[:, pl.ds(g * cols, cols)],
                dst.at[group],
                in_sem.at[t, group],
                g,
                t * GROUPS + g,
            )
    for g in range(GROUPS):
        scatter(limit_own, limit_in.at[group], in_sem.at[3, group], g, 3 * GROUPS + g)

    def compact(t, landed):
        for j in range(RING):
            arrived(landed.at[j], in_sem.at[t, j])
            wide[pl.ds(j * rows, rows), :] = landed[j].astype(jnp.float32)
        return wide[...].astype(jnp.bfloat16)

    def place(ab, values):
        return SLOT[ab[::-1]] if values else SLOT[ab]

    def have(ab, values):
        a, b = ab
        store, arrive, pair = (v_all, v_sem, v_pair_sem) if values else (k_all, k_sem, k_pair_sem)
        first, second = (1, 0) if values else (0, 1)
        p = place(ab, values)

        def whole(axis, step, to):
            s = place(to, values)
            send(store.at[2 * p], store.at[2 * s], arrive.at[s, 0], beside(axis, step))

        def part(axis, step, to, which):
            s = place(to, values)
            span = pl.ds(0, cut) if which == 0 else pl.ds(cut, keys - cut)
            send(
                store.at[2 * p, span],
                store.at[2 * s, span],
                arrive.at[s, which],
                beside(axis, step),
            )

        if b == 0:
            if a == 0:
                whole(first, 1, (3, 0))
                whole(first, -1, (1, 0))
            if a == 3:
                part(first, 1, (2, 0), 0)
            if a == 1:
                part(first, -1, (2, 0), 1)
            whole(second, 1, (a, 3))
            whole(second, -1, (a, 1))
        if b == 3:
            part(second, 1, (a, 2), 0)
        if b == 1:
            part(second, -1, (a, 2), 1)
        send(store.at[2 * p], store.at[2 * p + 1], pair.at[p], partner)

    def await_block(ab, values):
        a, b = ab
        store, arrive = (v_all, v_sem) if values else (k_all, k_sem)
        p = place(ab, values)
        if b == 2 or (b == 0 and a == 2):
            arrived(store.at[2 * p, pl.ds(0, cut)], arrive.at[p, 0])
            arrived(store.at[2 * p, pl.ds(cut, keys - cut)], arrive.at[p, 1])
        else:
            arrived(store.at[2 * p], arrive.at[p, 0])

    k_all[2 * SLOT[(0, 0)]] = compact(0, k_in)
    have((0, 0), False)
    v_all[2 * SLOT[(0, 0)]] = compact(1, v_in)
    have((0, 0), True)
    q_all[...] = compact(2, q_in)
    for j in range(RING):
        arrived(limit_in.at[j], in_sem.at[3, j])

    top[...] = jnp.full(top.shape, NEG, jnp.float32)
    total[...] = jnp.zeros(total.shape, jnp.float32)
    accum[...] = jnp.zeros(accum.shape, jnp.float32)
    factor = HEAD**-0.5 * math.log2(math.e)

    def bias_of(ab, other):
        x_at = lax.rem(x + ab[0], RING)
        y_at = lax.rem(y + ab[1], RING)
        core_at = 1 - core if other else core
        n = lax.broadcasted_iota(jnp.int32, (1, keys), 1)
        j = sum((n >= rows * i).astype(jnp.int32) for i in range(1, RING))
        holder = ((y_at * PLANES + 2 * j + lax.rem(x_at, 2)) * 2 + x_at // 2) * 2 + core_at
        pos = holder * rows + n - rows * j
        limit = limit_in[0, 0:1, :]
        limit = jnp.concatenate([limit, limit[:, : keys - 128]], axis=1)
        return jnp.where((pos >= text_slots) | (pos < limit), 0.0, NEG)

    def fold(at):
        for ab in BLOCKS[at * PER : (at + 1) * PER]:
            p = SLOT[ab]
            if ab != (0, 0) or True:
                arrived(k_all.at[2 * p + 1], k_pair_sem.at[p])
                arrived(v_all.at[2 * p + 1], v_pair_sem.at[p])
        bias = jnp.concatenate(
            [bias_of(ab, o) for ab in BLOCKS[at * PER : (at + 1) * PER] for o in range(2)], axis=1
        )
        span = pl.ds(at * PER * 2, PER * 2)
        many = PER * 2 * keys
        for h in range(MINE):
            lanes = slice(h * HEAD, (h + 1) * HEAD)
            kk = k_all[span, :, lanes].reshape(many, HEAD)
            vv = v_all[span, :, lanes].reshape(many, HEAD)
            scores = lax.dot_general(
                q_all[:, lanes], kk, (((1,), (1,)), ((), ())), preferred_element_type=jnp.float32
            )
            scores = scores * factor + bias
            old = top[h]
            new = jnp.maximum(old, jnp.max(scores, axis=1, keepdims=True))
            expo = jnp.exp2(scores - new[:, :1])
            shrink = jnp.exp2(old - new)
            top[h] = new
            total[h] = total[h] * shrink + jnp.sum(expo, axis=1, keepdims=True)
            accum[h] = accum[h] * shrink + jnp.dot(
                expo.astype(jnp.bfloat16), vv, preferred_element_type=jnp.float32
            )

    done = 0
    for n, ab in enumerate(ORDER):
        if n == 0:
            continue
        await_block(ab, False)
        have(ab, False)
        await_block(ab, True)
        have(ab, True)
        while (done + 1) * PER < len(BLOCKS) and READY[BLOCKS[(done + 1) * PER - 1]] < n:
            fold(done)
            done += 1
    while done * PER < len(BLOCKS):
        fold(done)
        done += 1

    for h in range(MINE):
        wide[:, pl.ds(h * HEAD, HEAD)] = accum[h] / total[h]
    for j in range(RING):
        o_out[j] = wide[pl.ds(j * rows, rows), :].astype(jnp.bfloat16)
    at_cols = pl.ds(pl.multiple_of(group * cols, cols), cols)
    for j in range(RING):
        scatter(o_out.at[j], attn.at[:, at_cols], o_sem.at[group], j, 4 * GROUPS + j)
    w_copy.wait()
    for g in range(GROUPS):
        arrived(attn.at[:, pl.ds(g * cols, cols)], o_sem.at[g])

    width = hidden_ref.shape[2]
    step = 512
    rate = jnp.zeros(speed.shape, jnp.float32)
    for at in range(0, width, step):
        lanes = slice(at, at + step)
        proj = jnp.dot(attn[...], w_out[:, lanes], preferred_element_type=jnp.float32)
        stream = residual_ref[:, lanes].astype(jnp.float32) + gate_ref[:, lanes] * proj
        stream = stream.astype(jnp.bfloat16)
        hidden_ref[0, :, lanes] = stream
        rate += lax.dot_general(
            stream,
            w_final_ref[:, lanes],
            (((1,), (1,)), ((), ())),
            preferred_element_type=jnp.float32,
        )
    speed[...] = rate
    to = device(2 * xh + 1 - cfg, y, z, core)
    send(speed, speed_in, speed_sem, to)
    arrived(speed_in, speed_sem)
    other = speed_in[...]
    cond = jnp.where(cfg == 0, rate, other)
    free = jnp.where(cfg == 0, other, rate)
    aligned[...] = jnp.zeros(aligned.shape, jnp.float32)
    aligned[pl.ds(0, rows), pl.ds(0, CH)] = free + 3.0 * (cond - free)
    rolled = pltpu.roll(aligned[...], lax.rem(rows * seq, 2 * PART), 0)
    parts = [rolled[i * PART : (i + 1) * PART] for i in range(4)]
    near = jnp.where(cfg == 0, parts[0], parts[1])
    far = jnp.where(cfg == 0, parts[2], parts[3])
    each = PLANES * 2
    base = core * RING * each
    own = base + seq // 2
    tiles[own] = (near + pltpu.roll(far, CH, 1)).astype(jnp.bfloat16)

    send(tiles.at[own], tiles.at[own], x_sem, across)
    arrived(tiles.at[base + y * each + 2 * z + 1 - xh], x_sem)
    both = tiles.at[pl.ds(base + y * each + 2 * z, 2)]
    for d, where in enumerate(planes):
        send(both, both, z_sem.at[d], where)
    for d in range(1, PLANES):
        z_at = lax.rem(z - d + PLANES, PLANES)
        arrived(tiles.at[pl.ds(base + y * each + 2 * z_at, 2)], z_sem.at[d - 1])
    plane = tiles.at[pl.ds(base + y * each, each)]
    for d in (2, 1, 3):
        send(plane, plane, y_sem.at[d], beside(1, d))
    send(plane, plane, core_sem.at[0], partner)
    for d in (1, 3, 2):
        y_at = lax.rem(y - d + RING, RING)
        plane = tiles.at[pl.ds(base + y_at * each, each)]
        arrived(plane, y_sem.at[d])
        send(plane, plane, core_sem.at[d], partner)
    for d in range(RING):
        y_at = lax.rem(y - d + RING, RING)
        arrived(tiles.at[pl.ds((1 - core) * RING * each + y_at * each, each)], core_sem.at[d])

    found = jnp.int32(0)
    for i in range(owner_ref.shape[0]):
        found = jnp.where(owner_ref[i] == seq, i, found)
    tile = text_slots // (2 * PART) + found
    first = tile * 2 * PART + PART * cfg

    def held(block):
        got = tiles[lax.rem(block, 2) * RING * each + block // 2].astype(jnp.float32)
        late = tile - rows * block // (2 * PART)
        return jnp.where(late == 0, got, pltpu.roll(got, CH, 1))

    begin = first // rows
    end = (first + PART - 1) // rows
    picked = held(begin)
    picked += jnp.where(end == begin, jnp.zeros_like(picked), held(end))
    for i in range(PART // 2):
        lanes = slice(2 * CH * i, 2 * CH * (i + 1))
        pair = [picked[2 * i + r : 2 * i + r + 1, :CH] for r in range(2)]
        latent_next_ref[:, lanes] = latent_ref[:, lanes] - 0.25 * jnp.concatenate(pair, axis=1)

    for copy in sent:
        copy.wait_send()
    for mine, copy in spread:

        @pl.when(jnp.logical_not(mine))
        def _():
            copy.wait_send()


def local(queries, keys, values, residual, gate, text_len, w_out, w_final, latent, owner):
    tokens, width = queries.shape[1:]
    nseq = lax.axis_size("seq")
    seqlen = tokens * nseq
    textslots = seqlen // 9
    cols = MINE * HEAD
    block = RING * tokens
    vmem = pl.BlockSpec(memory_space=pltpu.VMEM)
    bf16, f32 = jnp.bfloat16, jnp.float32
    dma = pltpu.SemaphoreType.DMA
    return pl.pallas_call(
        functools.partial(attention_kernel, textslots),
        out_shape=(
            jax.ShapeDtypeStruct(residual.shape, bf16),
            jax.ShapeDtypeStruct(latent.shape, f32),
        ),
        in_specs=[pl.BlockSpec(memory_space=pltpu.SMEM)] * 2
        + [vmem] * 5
        + [pl.BlockSpec(memory_space=pl.ANY), vmem, vmem],
        out_specs=(vmem, vmem),
        scratch_shapes=[
            pltpu.VMEM(w_out.shape, bf16),
            pltpu.VMEM((8, 128), jnp.int32),
            pltpu.VMEM((RING, 8, 128), jnp.int32),
            pltpu.VMEM((RING, tokens, cols), bf16),
            pltpu.VMEM((RING, tokens, cols), bf16),
            pltpu.VMEM((RING, tokens, cols), bf16),
            pltpu.VMEM((block, cols), f32),
            pltpu.VMEM((block, cols), bf16),
            pltpu.VMEM((2 * len(ORDER), block, cols), bf16),
            pltpu.VMEM((2 * len(ORDER), block, cols), bf16),
            pltpu.VMEM((MINE, block, HEAD), f32),
            pltpu.VMEM((MINE, block, HEAD), f32),
            pltpu.VMEM((MINE, block, HEAD), f32),
            pltpu.VMEM((RING, tokens, cols), bf16),
            pltpu.VMEM((tokens, width), bf16),
            pltpu.VMEM((tokens, CH), f32),
            pltpu.VMEM((tokens, CH), f32),
            pltpu.VMEM((4 * PART, 2 * CH), f32),
            pltpu.VMEM((nseq, PART, 2 * CH), bf16),
            dma,
            dma((88,)),
            dma((4, RING)),
            dma((20,)),
            dma((len(ORDER), 2)),
            dma((len(ORDER), 2)),
            dma((len(ORDER),)),
            dma((len(ORDER),)),
            dma((GROUPS,)),
            dma,
            dma,
            dma((PLANES - 1,)),
            dma((RING,)),
            dma((RING,)),
        ],
        compiler_params=pltpu.CompilerParams(
            collective_id=0, has_side_effects=True, vmem_limit_bytes=60 * 1024 * 1024
        ),
    )(text_len, owner, queries[0], keys[0], values[0], residual[0], gate, w_out, w_final.T, latent)


def solution(mesh):
    placed = (
        P("cfg", "seq", None),
        P("cfg", "seq", None),
        P("cfg", "seq", None),
        P("cfg", "seq", None),
        P("cfg", None),
        P("cfg"),
        P(),
        P(),
        P("seq", "cfg"),
        P(),
    )
    return jax.shard_map(
        local,
        mesh=mesh,
        in_specs=placed,
        out_specs=(P("cfg", "seq", None), P("seq", "cfg")),
        check_vma=False,
    )
```
